32 devices in a mesh: dp: 4 (over y, x), expert: 4 (over z), tensor: 2 (over core).
Axes of the slice: x: 2, y: 2, z: 4, core: 2. Of those that a mesh axis runs over, the one named last changes fastest.
Arguments:
- tokens: bfloat16 [2048, 7168], P(('dp', 'expert')), parts along dimension 0, may hold values from -6 to 6
- route_expert: int32 [2048, 8], P(('dp', 'expert')), parts along dimension 0, may hold values from 0 to 15, all different within a row; in each aligned block of 128 rows (0 to 127, 128 to 255, ...) at most 72 rows name the same one
- route_weight: int32 [2048, 8], P(('dp', 'expert')), parts along dimension 0, may hold values from 1 to 4095
- gate_weight: bfloat16 [16, 7168, 1024], P('expert', None, 'tensor'), may hold values from -0.0625 to 0.0625
- up_weight: bfloat16 [16, 7168, 1024], P('expert', None, 'tensor'), may hold values from -0.0625 to 0.0625
- down_weight: bfloat16 [16, 1024, 7168], P('expert', 'tensor'), may hold values from -0.1875 to 0.1875
- gate_scale: float32 [16, 1024], P('expert', 'tensor'), may hold values from 0.5 to 2
- up_scale: float32 [16, 1024], P('expert', 'tensor'), may hold values from 0.5 to 2
- down_scale: float32 [16, 7168], P('expert'), may hold values from 0.5 to 2
Outputs:
- combined: bfloat16 [2048, 7168], P(('dp', 'expert'), 'tensor'), parts along dimension 0
The draws below stay inside these ranges and needn't reach their ends.
There are 4 independent parts, one for each index of `dp`. The reference program is written for one: setup_inputs(seed, part) draws one part's arguments, and reference() takes and returns one part's arrays. A program takes and returns all parts, laid end to end along the dimension named above; an argument that names none is the same for every part. Nothing has to cross between parts.
Inputs may be any that keep to these rules, and one draw needn't show every extreme that they name: `route_expert`: within the 128 rows of one index of expert each expert is named at most 72 times, a bound that some block reaches; a token names 8 different experts.
All inputs are finite; a program needn't handle non-finite values.
Results may differ from the reference program's by a relative error of at most 0.0057.
Values may be sent and summed in bfloat16 or wider, within the bound.
No kernel may reach another device: no remote copies, remote signals or barrier semaphores. Data moves between devices by JAX's collectives and lax.ppermute only.
A program may use at most 256 MiB of HBM per device.

```python
import math
import jax
import jax.numpy as jnp
import numpy as np
from jax import lax

D = 7168
FF = 1024
TOP = 8
EXPERTS = 16
TOK_DEV = 128
CAP = 72
TOKENS = 512
N_EXPERT = 4


def set_ends(result, key, low, largest):
    extent = result.shape
    place = [jax.random.randint(jax.random.fold_in(key, axis), (), 0, extent[axis]) for axis in range(len(extent))]
    result = result.at[tuple(place)].set(low)
    longest = extent.index(max(extent))
    place[longest] = (place[longest] + 1) % extent[longest]
    return result.at[tuple(place)].set(largest)


def shard_levels(own_key, shape, split, least, top_value):
    level = 1.0
    for dim, blocks in split:
        steps = jax.random.uniform(jax.random.fold_in(jax.random.fold_in(own_key, 6), dim), (blocks,), jnp.float32, least / len(split), top_value / len(split))
        level = level * jnp.repeat(jnp.exp(steps), shape[dim] // blocks).reshape((-1,) + (1,) * (len(shape) - 1 - dim))
    return level


def shared_out(stream_key, own, number, rows, number_of, top, most, skew):
    order = jax.random.permutation(stream_key, number_of)
    heavy_load, usual = portions_of(number_of, rows * top, most, skew, True), portions_of(number_of, rows * top, most, skew, False)
    places = jnp.arange(number_of)

    def named(sizes, offset_by):
        used = int((sizes > 0).sum())
        fixed = max(1, used // 4)
        passed = fixed + (places - fixed + offset_by * (used - fixed)) % max(1, number_of - fixed)
        return jnp.zeros((number_of,), jnp.int32).at[order[jnp.where(places < fixed, places, passed)]].set(jnp.asarray(sizes, jnp.int32))

    sizes = jnp.where(number % 4 == 0, named(heavy_load, number // 4), named(usual, number - number // 4 - 1))
    mixed = jax.random.permutation(jax.random.fold_in(own, 3), number_of)
    donor, taker = mixed[0:number_of // 2 * 2:2], mixed[1:number_of // 2 * 2:2]
    room = jnp.minimum(sizes[donor] - 1, most - sizes[taker]) // 2
    room = jnp.where((donor == order[0]) | (taker == order[0]) | (sizes[taker] == 0), 0, jnp.maximum(room, 0))
    passed = jax.random.randint(jax.random.fold_in(own, 4), (number_of // 2,), 0, 1 << 20) % (room + 1)
    sizes = sizes.at[donor].add(-passed).at[taker].add(passed)
    labels = jnp.searchsorted(jnp.cumsum(sizes), jnp.arange(rows * top), side="right").astype(jnp.int32)
    table = labels.reshape(top, rows).T
    table = table[jax.random.permutation(jax.random.fold_in(own, 1), rows)]
    offset_by = jax.random.randint(jax.random.fold_in(own, 2), (rows, 1), 0, top)
    return jnp.take_along_axis(table, (jnp.arange(top)[None, :] + offset_by) % top, axis=1)


def portions_of(count, total, reach, skew, full):
    weights = [(1 << 20) // math.isqrt(grade ** skew) + 1 for grade in range(1, count + 1)]
    largest = reach if full else min(reach, max(-(-total // count), total * weights[0] // sum(weights)))
    least = 1 if total - largest >= count - 1 else 0
    counts, spare = [largest] + [least] * (count - 1), total - largest - least * (count - 1)
    while spare > 0:
        candidates = [i for i in range(1, count) if counts[i] < largest] or [i for i in range(1, count) if counts[i] < reach]
        pool, remaining = sum([weights[i] for i in candidates]), spare
        for i in candidates:
            more = min(reach - counts[i], max(1, remaining * weights[i] // pool), spare)
            counts[i] = counts[i] + more
            spare = spare - more
    return np.array(counts)


def bell_draw(rng, dims, spread, reach, shards=(), kind=jnp.bfloat16):
    array = spread * jax.random.normal(rng, dims, jnp.float32)
    if shards:
        array = array * shard_levels(rng, dims, shards, -0.22, 0.18)
    return jnp.clip(array, -reach, reach).astype(kind)


def setup_inputs(seed: int = 0, part: int = 0) -> dict:
    key_of = jax.random.split(jax.random.key(seed), 10)
    part_keys = jax.random.split(jax.random.fold_in(key_of[9], part), 10)
    tokens = bell_draw(part_keys[0], (TOKENS, D), 1.0, 6.0, ((0, 4),))
    route_expert_keys = jax.random.split(jax.random.fold_in(part_keys[1], 1), TOKENS // TOK_DEV)
    route_expert_turns = jax.random.permutation(jax.random.fold_in(part_keys[1], 3), TOKENS // TOK_DEV)
    route_expert = jax.vmap(lambda own, number: shared_out(jax.random.fold_in(part_keys[1], 2), own, number, TOK_DEV, EXPERTS, TOP, CAP, 2))(route_expert_keys, route_expert_turns).reshape((TOKENS, TOP))
    route_weight = set_ends(jax.random.randint(part_keys[2], (TOKENS, TOP), 1, 4096), jax.random.fold_in(part_keys[2], 1), 1, 4095).astype(jnp.int32)
    gate_weight = bell_draw(key_of[3], (EXPERTS, D, FF), D ** -0.5, 0.0625, ((0, 4), (2, 2)))
    up_weight = bell_draw(key_of[4], (EXPERTS, D, FF), D ** -0.5, 0.0625, ((0, 4), (2, 2)))
    down_weight = bell_draw(key_of[5], (EXPERTS, FF, D), FF ** -0.5, 0.1875, ((0, 4), (1, 2)))
    gate_scale = jnp.clip(jnp.exp(math.log(2.0) - 1.3862944 * jax.random.uniform(key_of[6], (EXPERTS, FF), jnp.float32) ** shard_levels(key_of[6], (EXPERTS, FF), ((0, 4), (1, 2)), -0.2, 0.2)), 0.5, 2.0)
    up_scale = jnp.clip(jnp.exp(math.log(2.0) - 1.3862944 * jax.random.uniform(key_of[7], (EXPERTS, FF), jnp.float32) ** shard_levels(key_of[7], (EXPERTS, FF), ((0, 4), (1, 2)), -0.2, 0.2)), 0.5, 2.0)
    down_scale = jnp.clip(jnp.exp(math.log(2.0) - 1.3862944 * jax.random.uniform(key_of[8], (EXPERTS, D), jnp.float32) ** shard_levels(key_of[8], (EXPERTS, D), ((0, 4),), -0.2, 0.2)), 0.5, 2.0)
    return {"tokens": tokens, "route_expert": route_expert, "route_weight": route_weight, "gate_weight": gate_weight, "up_weight": up_weight, "down_weight": down_weight, "gate_scale": gate_scale, "up_scale": up_scale, "down_scale": down_scale}


ROUTE_SCALE = 2.5


def slot_numbers(route_block, experts):
    flat_ids = route_block.reshape(-1).astype(jnp.int32)
    one_hot = (flat_ids[:, None] == jnp.arange(experts, dtype=jnp.int32)[None, :]).astype(jnp.int32)
    earlier = (jnp.cumsum(one_hot, axis=0) - one_hot).astype(jnp.int32)
    return jnp.sum(earlier * one_hot, axis=1).astype(jnp.int32).reshape(route_block.shape)


def reference(tokens, route_expert, route_weight, gate_weight, up_weight, down_weight, gate_scale, up_scale, down_scale):
    blocks = N_EXPERT
    total_rows = TOK_DEV * blocks
    route_blocks = route_expert.reshape(blocks, TOK_DEV, TOP)

    def block_slots(block_ids):
        return slot_numbers(block_ids, EXPERTS)

    slots = jax.vmap(block_slots)(route_blocks).reshape(total_rows, TOP).astype(jnp.int32)
    block_of = (jnp.arange(total_rows, dtype=jnp.int32) // TOK_DEV)[:, None]
    target = (route_expert.astype(jnp.int32) * (blocks * CAP) + block_of * CAP + slots).astype(jnp.int32)
    token_ids = jnp.repeat(jnp.arange(total_rows, dtype=jnp.int32), TOP)
    table = jnp.full((EXPERTS * blocks * CAP,), total_rows, jnp.int32).at[target.reshape(-1)].set(token_ids)
    padded = jnp.concatenate([tokens, jnp.zeros((1, D), jnp.bfloat16)], axis=0)

    def one_expert(operands):
        index_row, w_gate, w_up, w_down, s_gate, s_up, s_down = operands
        rows_in = padded[index_row]
        gate_act = jnp.dot(rows_in, w_gate, preferred_element_type=jnp.float32) * s_gate[None, :]
        up_act = jnp.dot(rows_in, w_up, preferred_element_type=jnp.float32) * s_up[None, :]
        hidden = (jax.nn.silu(gate_act) * up_act).astype(jnp.bfloat16)
        return (jnp.dot(hidden, w_down, preferred_element_type=jnp.float32) * s_down[None, :]).astype(jnp.bfloat16)

    outputs = lax.map(one_expert, (table.reshape(EXPERTS, blocks * CAP), gate_weight, up_weight, down_weight, gate_scale, up_scale, down_scale))
    flat_out = outputs.reshape(EXPERTS * blocks * CAP, D)
    weights_f = route_weight.astype(jnp.float32)
    mix = ROUTE_SCALE * weights_f / jnp.sum(weights_f, axis=1, keepdims=True)
    combined = jnp.zeros((total_rows, D), jnp.float32)
    for route_slot in range(TOP):
        combined = combined + mix[:, route_slot:route_slot + 1] * flat_out[target[:, route_slot]].astype(jnp.float32)
    return combined.astype(jnp.bfloat16)
```

```python
import functools

import jax
import jax.numpy as jnp
from jax import lax
from jax.experimental import pallas as pl
from jax.experimental.pallas import tpu as pltpu
from jax.sharding import PartitionSpec as P

ROUTE_SCALE = 2.5
UNIT = 256
ROW_LIMIT = 512


def split_units(total, shares):
    units = total // UNIT
    whole = sum(shares)
    ends = [round(units * sum(shares[: i + 1]) / whole) for i in range(len(shares))]
    starts = [0] + ends[:-1]
    return [(a * UNIT, (b - a) * UNIT) for a, b in zip(starts, ends) if b > a]


def gate_up_kernel(
    groups, tok, row0, col0, width, tile, widths, first, last, depth, *refs
):
    refs = list(refs)
    reach_ref, tok_ref = refs[:2]
    pos = 2
    direct, passed = [], []
    for _ in widths:
        direct.append(refs[pos : pos + groups - 1])
        pos += groups - 1
        passed.append(refs[pos : pos + groups - 1])
        pos += groups - 1
    gate_ref, up_ref = refs[pos : pos + 2]
    pos += 2
    if not first:
        sum_in = refs[pos]
        pos += 1
    if last:
        gate_scale_ref, up_scale_ref = refs[pos : pos + 2]
        pos += 2
    out_ref = refs[pos]
    rows_v, wbuf, row_sem, w_sem = refs[pos + 1 :]

    e = pl.program_id(0)
    count = gate_ref.shape[0]
    feats = gate_ref.shape[2]
    steps = width // tile

    def weight_copies(flat):
        slot = lax.rem(flat, depth)
        which, step = lax.div(flat, steps), lax.rem(flat, steps)
        start = pl.multiple_of(col0 + step * tile, tile if col0 % tile == 0 else UNIT)
        return [
            pltpu.make_async_copy(
                src.at[which, pl.ds(start, tile)], wbuf.at[slot, i], w_sem.at[slot, i]
            )
            for i, src in enumerate((gate_ref, up_ref))
        ]

    def row_copies():
        own = pltpu.make_async_copy(
            tok_ref.at[pl.ds(row0, tok), pl.ds(col0, width)],
            rows_v.at[pl.ds(0, tok)],
            row_sem.at[0, 0],
        )
        pairs = []
        for p in range(1, groups):
            at = 0
            for i, w in enumerate(widths):
                dst = rows_v.at[pl.ds(p * tok, tok), pl.ds(at, w)]
                sem = row_sem.at[p, i]
                pairs.append(
                    (
                        p,
                        pltpu.make_async_copy(direct[i][p - 1], dst, sem),
                        pltpu.make_async_copy(passed[i][groups - p - 1], dst, sem),
                    )
                )
                at += w
        return own, pairs

    @pl.when(e == 0)
    def _():
        own, pairs = row_copies()
        own.start()
        for c in weight_copies(0):
            c.start()
        for p, a, b in pairs:
            near = reach_ref[0] >= p

            @pl.when(near)
            def _():
                a.start()

            @pl.when(jnp.logical_not(near))
            def _():
                b.start()

        for f in range(1, min(depth - 1, count * steps)):
            for c in weight_copies(f):
                c.start()
        own.wait()
        for p, a, b in pairs:
            a.wait()

    sums = [None, None]
    for t in range(steps):
        flat = e * steps + t
        ahead = flat + depth - 1

        @pl.when(ahead < count * steps)
        def _():
            for c in weight_copies(ahead):
                c.start()

        x = rows_v[:, t * tile : (t + 1) * tile]
        slot = lax.rem(flat, depth)
        for i, c in enumerate(weight_copies(flat)):
            c.wait()
            part = jnp.dot(x, wbuf[slot, i], preferred_element_type=jnp.float32)
            sums[i] = part if sums[i] is None else sums[i] + part
    if not first:
        sums = [
            s + sum_in[0, :, i * feats : (i + 1) * feats] for i, s in enumerate(sums)
        ]
    if last:
        gate = sums[0] * gate_scale_ref[0]
        up = sums[1] * up_scale_ref[0]
        out_ref[0] = ((gate / (1.0 + jnp.exp(-gate))) * up).astype(jnp.bfloat16)
    else:
        for i, s in enumerate(sums):
            out_ref[0, :, i * feats : (i + 1) * feats] = s


def gate_up(
    reach, tokens, direct, passed, weights, scales, sums, row0, tok, col0, widths, last, tile
):
    gate_w, up_w = weights
    count, _, feats = gate_w.shape
    groups = len(direct[0]) + 1
    rows = groups * tok
    width = sum(widths)
    first = sums is None
    while width % tile:
        tile -= UNIT
    depth = 4
    any_spec = pl.BlockSpec(memory_space=pl.ANY)
    operands = [reach, tokens]
    specs = [pl.BlockSpec(memory_space=pltpu.SMEM), any_spec]
    for a, b in zip(direct, passed):
        operands += list(a) + list(b)
        specs += [any_spec] * (len(a) + len(b))
    operands += [gate_w, up_w]
    specs += [any_spec, any_spec]
    if not first:
        operands.append(sums)
        specs.append(pl.BlockSpec((1, rows, 2 * feats), lambda e: (e, 0, 0)))
    if last:
        operands += [s.reshape(count, 1, feats) for s in scales]
        specs += [pl.BlockSpec((1, 1, feats), lambda e: (e, 0, 0))] * 2
        out_shape = jax.ShapeDtypeStruct((count, rows, feats), jnp.bfloat16)
        out_spec = pl.BlockSpec((1, rows, feats), lambda e: (e, 0, 0))
    else:
        out_shape = jax.ShapeDtypeStruct((count, rows, 2 * feats), jnp.float32)
        out_spec = pl.BlockSpec((1, rows, 2 * feats), lambda e: (e, 0, 0))
    return pl.pallas_call(
        functools.partial(
            gate_up_kernel, groups, tok, row0, col0, width, tile, tuple(widths), first, last, depth
        ),
        grid=(count,),
        in_specs=specs,
        out_specs=out_spec,
        out_shape=out_shape,
        scratch_shapes=[
            pltpu.VMEM((rows, width), jnp.bfloat16),
            pltpu.VMEM((depth, 2, tile, feats), jnp.bfloat16),
            pltpu.SemaphoreType.DMA((groups, len(widths))),
            pltpu.SemaphoreType.DMA((depth, 2)),
        ],
        compiler_params=pltpu.CompilerParams(vmem_limit_bytes=60 << 20),
        cost_estimate=pl.CostEstimate(
            flops=4 * count * rows * width * feats,
            bytes_accessed=4 * count * width * feats + 2 * rows * width,
            transcendentals=0,
        ),
        name="gate_up",
    )(*operands)


def down_kernel(groups, cores, tok, cols, half, *refs):
    h_ref, w_ref, scale_ref, mix_ref, own_ref, rest_ref, hv, wv, yv, h_sem, w_sem, y_sem = refs
    count, rows, _ = h_ref.shape
    col0, width = cols
    w_copies = [
        [
            pltpu.make_async_copy(
                w_ref.at[e, :, pl.ds(c * half + col0, width)], wv.at[c, e], w_sem.at[c, e]
            )
            for e in range(count)
        ]
        for c in range(cores)
    ]
    h_copies = [
        pltpu.make_async_copy(h_ref.at[e], hv.at[e], h_sem.at[e]) for e in range(count)
    ]
    for e in range(count):
        h_copies[e].start()
        w_copies[0][e].start()
    for c in range(1, cores):
        for e in range(count):
            w_copies[c][e].start()
    out_copies = []
    for c in range(cores):
        total = None
        for e in range(count):
            if c == 0:
                h_copies[e].wait()
            w_copies[c][e].wait()
            part = jnp.dot(hv[e], wv[c, e], preferred_element_type=jnp.float32)
            scale = scale_ref[e : e + 1, c * half + col0 : c * half + col0 + width]
            part = part * scale * mix_ref[:, e : e + 1]
            total = part if total is None else total + part
        yv[c] = total.astype(jnp.bfloat16).reshape(groups, tok, width)
        out_copies.append(pltpu.make_async_copy(yv.at[c, 0], own_ref.at[c], y_sem.at[c, 0]))
        out_copies[-1].start()
        for p in range(1, groups):
            out_copies.append(
                pltpu.make_async_copy(yv.at[c, p], rest_ref.at[p - 1, c], y_sem.at[c, p])
            )
            out_copies[-1].start()
    for c in out_copies:
        c.wait()


def down(hidden, down_w, scale, mix, groups, cores, tok, cols):
    count, rows, feats = hidden.shape
    half = down_w.shape[2] // cores
    width = cols[1]
    any_spec = pl.BlockSpec(memory_space=pl.ANY)
    vmem = pl.BlockSpec(memory_space=pltpu.VMEM)
    return pl.pallas_call(
        functools.partial(down_kernel, groups, cores, tok, cols, half),
        in_specs=[any_spec, any_spec, vmem, vmem],
        out_specs=[any_spec, any_spec],
        out_shape=[
            jax.ShapeDtypeStruct((cores, tok, width), jnp.bfloat16),
            jax.ShapeDtypeStruct((groups - 1, cores, tok, width), jnp.bfloat16),
        ],
        scratch_shapes=[
            pltpu.VMEM((count, rows, feats), jnp.bfloat16),
            pltpu.VMEM((cores, count, feats, width), jnp.bfloat16),
            pltpu.VMEM((cores, groups, tok, width), jnp.bfloat16),
            pltpu.SemaphoreType.DMA((count,)),
            pltpu.SemaphoreType.DMA((cores, count)),
            pltpu.SemaphoreType.DMA((cores, groups)),
        ],
        compiler_params=pltpu.CompilerParams(vmem_limit_bytes=60 << 20),
        cost_estimate=pl.CostEstimate(
            flops=2 * count * rows * feats * width * cores,
            bytes_accessed=2 * count * feats * width * cores + 2 * rows * width * cores,
            transcendentals=0,
        ),
        name="down",
    )(hidden, down_w, scale, mix)


def body(
    gather_shares,
    matmul_runs,
    return_shares,
    parts,
    tokens,
    route_expert,
    route_weight,
    gate_weight,
    up_weight,
    down_weight,
    gate_scale,
    up_scale,
    down_scale,
):
    tok_rows, model_width = tokens.shape
    groups = lax.axis_size("expert")
    cores = lax.axis_size("tensor")
    assert cores == 2
    local_experts = gate_weight.shape[0]
    experts = local_experts * groups
    half_width = model_width // cores
    z, core = lax.axis_index("expert"), lax.axis_index("tensor")
    both = ("expert", "tensor")
    while groups * tok_rows // parts > ROW_LIMIT and tok_rows % (2 * parts) == 0:
        parts *= 2
    tok = tok_rows // parts
    if groups > 4:
        gather_shares, matmul_runs = (1, 1), (1, 1)

    def other_core(value):
        return lax.ppermute(value, "tensor", [(0, 1), (1, 0)])

    def onward(value, ups, downs):
        pairs = [(2 * i, 2 * (i + 1)) for i in ups] + [(2 * i + 1, 2 * (i - 1) + 1) for i in downs]
        return lax.ppermute(value, both, pairs)

    reach = jnp.where(core == 0, z, groups - 1 - z).astype(jnp.int32)

    weights_f = route_weight.astype(jnp.float32)
    mix = ROUTE_SCALE * weights_f / jnp.sum(weights_f, axis=1, keepdims=True)
    chosen = route_expert[:, :, None] == jnp.arange(experts, dtype=jnp.int32)[None, None, :]
    mix_rows = jnp.sum(jnp.where(chosen, mix[:, :, None], 0.0), axis=1)
    mix_all = lax.all_gather(mix_rows, "expert", axis=0, tiled=False)
    mix_all = lax.dynamic_slice_in_dim(mix_all, z * local_experts, local_experts, 2)
    turn = jnp.where(core == 0, groups - 1, 1)
    order = (z + turn * jnp.arange(groups, dtype=jnp.int32)) % groups
    mix_all = mix_all[order]

    chunks = split_units(model_width, gather_shares)
    ret_chunks = split_units(half_width, return_shares)
    outs = []
    for part in range(parts):
        row0 = part * tok
        direct = [[] for _ in chunks]
        passed = [[] for _ in chunks]
        for k, (at, w) in enumerate(chunks):
            held = tokens[row0 : row0 + tok, at : at + w]
            for s in range(1, groups):
                held = onward(held, range(s - 1, groups - 1), range(1, groups - s + 1))
                direct[k].append(held)
                passed[k].append(other_core(held))
        sums, done = None, 0
        for i, run in enumerate(matmul_runs):
            last = i == len(matmul_runs) - 1
            ks = range(done, min(done + run, len(chunks)))
            sums = gate_up(
                reach.reshape(1),
                tokens,
                [direct[k] for k in ks],
                [passed[k] for k in ks],
                (gate_weight, up_weight),
                (gate_scale, up_scale),
                sums,
                row0,
                tok,
                chunks[done][0],
                [chunks[k][1] for k in ks],
                last,
                1792,
            )
            done += run
        hidden = sums
        mix_part = mix_all[:, row0 : row0 + tok].reshape(groups * tok, local_experts)
        pieces = []
        for cols in ret_chunks:
            own, rest = down(
                hidden, down_weight, down_scale, mix_part, groups, cores, tok, cols
            )
            other = other_core(rest)

            def both_cores(s):
                return rest[s - 1].astype(jnp.float32) + other[groups - s - 1].astype(jnp.float32)

            total = both_cores(1)
            for s in range(1, groups):
                arrived = onward(
                    total.astype(jnp.bfloat16), range(0, s), range(groups - s, groups)
                ).astype(jnp.float32)
                total = arrived + (both_cores(s + 1) if s < groups - 1 else own.astype(jnp.float32))
            give = jnp.where(core == 0, total[1], total[0]).astype(jnp.bfloat16)
            keep = jnp.where(core == 0, total[0], total[1])
            pieces.append((keep + other_core(give).astype(jnp.float32)).astype(jnp.bfloat16))
        outs.append(jnp.concatenate(pieces, axis=1))
    return jnp.concatenate(outs, axis=0) if parts > 1 else outs[0]


def solution(mesh):
    in_specs = (
        P(("dp", "expert"), None),
        P(("dp", "expert"), None),
        P(("dp", "expert"), None),
        P("expert", None, "tensor"),
        P("expert", None, "tensor"),
        P("expert", "tensor", None),
        P("expert", "tensor"),
        P("expert", "tensor"),
        P("expert", None),
    )
    out_specs = P(("dp", "expert"), "tensor")
    plan = functools.partial(body, (1, 1, 1, 1), (3, 1), (2, 4, 4, 4), 1)
    return jax.shard_map(plan, mesh=mesh, in_specs=in_specs, out_specs=out_specs, check_vma=False)
```

```python
import functools

import jax
import jax.numpy as jnp
from jax import lax
from jax.experimental import pallas as pl
from jax.experimental.pallas import tpu as pltpu
from jax.sharding import PartitionSpec as P


ROUTE_SCALE = 2.5
UNIT = 256
ROW_BLOCKS = 1
PIECE = 2048
ROW_LIMIT = 512


PARTS = 1
GATHER = (4, 4, 3, 3)
RUNS = (1, 3)
RETURN = (4, 5, 5)
RING_FROM = 0


def split_units(total, shares):
    units = total // UNIT
    whole = sum(shares)
    ends = [round(units * sum(shares[: i + 1]) / whole) for i in range(len(shares))]
    starts = [0] + ends[:-1]
    return [(a * UNIT, (b - a) * UNIT) for a, b in zip(starts, ends) if b > a]


def gate_up_kernel(
    groups, tok, row0, col0, width, tile, widths, first, last, depth, *refs
):
    refs = list(refs)
    reach_ref, tok_ref = refs[:2]
    pos = 2
    direct, passed = [], []
    for _ in widths:
        direct.append(refs[pos : pos + groups - 1])
        pos += groups - 1
        passed.append(refs[pos : pos + groups - 1])
        pos += groups - 1
    gate_ref, up_ref = refs[pos : pos + 2]
    pos += 2
    if not first:
        sum_in = refs[pos]
        pos += 1
    if last:
        gate_scale_ref, up_scale_ref = refs[pos : pos + 2]
        pos += 2
    out_ref = refs[pos]
    rows_v, wbuf, row_sem, w_sem = refs[pos + 1 :]

    e = pl.program_id(0)
    count = gate_ref.shape[0]
    feats = gate_ref.shape[2]
    steps = width // tile
    total = 2 * count * steps

    def weight_copy(which, step, i, slot):
        src = (gate_ref, up_ref)[i]
        return pltpu.make_async_copy(
            src.at[which, pl.ds(col0 + step * tile, tile)], wbuf.at[slot], w_sem.at[slot]
        )

    def place(flat):
        which, inner = divmod(flat, 2 * steps)
        return which, inner // 2, inner % 2

    def row_copies():
        own = pltpu.make_async_copy(
            tok_ref.at[pl.ds(row0, tok), pl.ds(col0, width)],
            rows_v.at[pl.ds(0, tok)],
            row_sem.at[0, 0],
        )
        pairs = []
        for p in range(1, groups):
            at = 0
            for i, w in enumerate(widths):
                dst = rows_v.at[pl.ds(p * tok, tok), pl.ds(at, w)]
                sem = row_sem.at[p, i]
                pairs.append(
                    (
                        p,
                        pltpu.make_async_copy(direct[i][p - 1], dst, sem),
                        pltpu.make_async_copy(passed[i][groups - p - 1], dst, sem),
                    )
                )
                at += w
        return own, pairs

    @pl.when(e == 0)
    def _():
        own, pairs = row_copies()
        own.start()
        for p, a, b in pairs:
            near = reach_ref[0] >= p

            @pl.when(near)
            def _():
                a.start()

            @pl.when(jnp.logical_not(near))
            def _():
                b.start()

        for f in range(min(depth - 1, total)):
            weight_copy(*place(f), f % depth).start()
        own.wait()
        for p, a, b in pairs:
            a.wait()

    sums = [None, None]
    for inner in range(2 * steps):
        flat = e * (2 * steps) + inner
        ahead = inner + depth - 1
        over, at = ahead // (2 * steps), ahead % (2 * steps)

        @pl.when(e + over < count)
        def _():
            weight_copy(e + over, at // 2, at % 2, lax.rem(flat + depth - 1, depth)).start()

        t, i = inner // 2, inner % 2
        slot = lax.rem(flat, depth)
        weight_copy(e, t, i, slot).wait()
        part = jnp.dot(
            rows_v[:, t * tile : (t + 1) * tile], wbuf[slot], preferred_element_type=jnp.float32
        )
        sums[i] = part if sums[i] is None else sums[i] + part
    if not first:
        sums = [
            s + sum_in[0, :, i * feats : (i + 1) * feats] for i, s in enumerate(sums)
        ]
    if last:
        gate = sums[0] * gate_scale_ref[pl.ds(e, 1), :]
        up = sums[1] * up_scale_ref[pl.ds(e, 1), :]
        out_ref[0] = ((gate / (1.0 + jnp.exp(-gate))) * up).astype(jnp.bfloat16)
    else:
        for i, s in enumerate(sums):
            out_ref[0, :, i * feats : (i + 1) * feats] = s


def gate_up(
    reach, tokens, direct, passed, weights, scales, sums, row0, tok, col0, widths, last, tile
):
    gate_w, up_w = weights
    count, _, feats = gate_w.shape
    groups = len(direct[0]) + 1
    rows = groups * tok
    width = sum(widths)
    first = sums is None
    while width % tile:
        tile -= UNIT
    depth = max(4, min(8, (14 << 20) // (2 * tile * feats)))
    any_spec = pl.BlockSpec(memory_space=pl.ANY)
    operands = [reach, tokens]
    specs = [pl.BlockSpec(memory_space=pltpu.SMEM), any_spec]
    for a, b in zip(direct, passed):
        operands += list(a) + list(b)
        specs += [any_spec] * (len(a) + len(b))
    operands += [gate_w, up_w]
    specs += [any_spec, any_spec]
    if not first:
        operands.append(sums)
        specs.append(pl.BlockSpec((1, rows, 2 * feats), lambda e: (e, 0, 0)))
    if last:
        operands += list(scales)
        specs += [pl.BlockSpec((count, feats), lambda e: (0, 0))] * 2
        out_shape = jax.ShapeDtypeStruct((count, rows, feats), jnp.bfloat16)
        out_spec = pl.BlockSpec((1, rows, feats), lambda e: (e, 0, 0))
    else:
        out_shape = jax.ShapeDtypeStruct((count, rows, 2 * feats), jnp.float32)
        out_spec = pl.BlockSpec((1, rows, 2 * feats), lambda e: (e, 0, 0))
    return pl.pallas_call(
        functools.partial(
            gate_up_kernel, groups, tok, row0, col0, width, tile, tuple(widths), first, last, depth
        ),
        grid=(count,),
        in_specs=specs,
        out_specs=out_spec,
        out_shape=out_shape,
        scratch_shapes=[
            pltpu.VMEM((rows, width), jnp.bfloat16),
            pltpu.VMEM((depth, tile, feats), jnp.bfloat16),
            pltpu.SemaphoreType.DMA((groups, len(widths))),
            pltpu.SemaphoreType.DMA((depth,)),
        ],
        compiler_params=pltpu.CompilerParams(vmem_limit_bytes=60 << 20),
        cost_estimate=pl.CostEstimate(
            flops=4 * count * rows * width * feats,
            bytes_accessed=4 * count * width * feats + 2 * rows * width,
            transcendentals=0,
        ),
        name="gate_up",
    )(*operands)


def down_kernel(groups, cores, tok, cols, half, pieces, *refs):
    h_ref, w_ref, scale_ref, mix_ref, own_ref, keep_ref, send_ref, hv, wv, yv, h_sem, w_sem, y_sem = refs
    count, rows, _ = h_ref.shape
    col0, _ = cols
    h_copies = [
        pltpu.make_async_copy(h_ref.at[e], hv.at[e], h_sem.at[e]) for e in range(count)
    ]
    spans = [(c, at, w) for c in range(cores) for at, w in pieces]
    w_copies = [
        [
            pltpu.make_async_copy(
                w_ref.at[e, :, pl.ds(c * half + col0 + at, w)],
                wv.at[c, e, :, pl.ds(at, w)],
                w_sem.at[i, e],
            )
            for e in range(count)
        ]
        for i, (c, at, w) in enumerate(spans)
    ]
    for e in range(count):
        h_copies[e].start()
        w_copies[0][e].start()
    for group in w_copies[1:]:
        for c in group:
            c.start()
    out_copies = []
    for i, (c, at, w) in enumerate(spans):
        lo = c * half + col0 + at
        block = rows // ROW_BLOCKS
        for r in range(ROW_BLOCKS):
            total = None
            for e in range(count):
                if r == 0:
                    if i == 0:
                        h_copies[e].wait()
                    w_copies[i][e].wait()
                part = jnp.dot(
                    hv[e, r * block : (r + 1) * block],
                    wv[c, e, :, at : at + w],
                    preferred_element_type=jnp.float32,
                )
                mixed = mix_ref[r * block : (r + 1) * block, e : e + 1]
                part = part * scale_ref[e : e + 1, lo : lo + w] * mixed
                total = part if total is None else total + part
            yv[c, r * block : (r + 1) * block, at : at + w] = total.astype(jnp.bfloat16)
        here = pl.ds(at, w)
        moves = [(own_ref.at[c, :, here], 0)]
        for p in range(1, groups):
            moves.append((keep_ref.at[groups - p - 1, c, :, here], p))
            moves.append((send_ref.at[p - 1, c, :, here], p))
        for n, (dst, p) in enumerate(moves):
            copy = pltpu.make_async_copy(
                yv.at[c, pl.ds(p * tok, tok), here], dst, y_sem.at[i, n]
            )
            copy.start()
            out_copies.append(copy)
    for c in out_copies:
        c.wait()


def down(hidden, down_w, scale, mix, groups, cores, tok, cols):
    count, rows, feats = hidden.shape
    half = down_w.shape[2] // cores
    width = cols[1]
    pieces = [(at, min(PIECE, width - at)) for at in range(0, width, PIECE)]
    any_spec = pl.BlockSpec(memory_space=pl.ANY)
    vmem = pl.BlockSpec(memory_space=pltpu.VMEM)
    return pl.pallas_call(
        functools.partial(down_kernel, groups, cores, tok, cols, half, pieces),
        in_specs=[any_spec, any_spec, vmem, vmem],
        out_specs=[any_spec] * 3,
        out_shape=[
            jax.ShapeDtypeStruct((cores, tok, width), jnp.bfloat16),
            jax.ShapeDtypeStruct((groups - 1, cores, tok, width), jnp.bfloat16),
            jax.ShapeDtypeStruct((groups - 1, cores, tok, width), jnp.bfloat16),
        ],
        scratch_shapes=[
            pltpu.VMEM((count, rows, feats), jnp.bfloat16),
            pltpu.VMEM((cores, count, feats, width), jnp.bfloat16),
            pltpu.VMEM((cores, rows, width), jnp.bfloat16),
            pltpu.SemaphoreType.DMA((count,)),
            pltpu.SemaphoreType.DMA((cores * len(pieces), count)),
            pltpu.SemaphoreType.DMA((cores * len(pieces), 2 * groups - 1)),
        ],
        compiler_params=pltpu.CompilerParams(vmem_limit_bytes=60 << 20),
        cost_estimate=pl.CostEstimate(
            flops=2 * count * rows * feats * width * cores,
            bytes_accessed=2 * count * feats * width * cores + 2 * rows * width * cores,
            transcendentals=0,
        ),
        name="down",
    )(hidden, down_w, scale, mix)


def layer(
    gather_shares,
    matmul_runs,
    return_shares,
    ring_from,
    parts,
    tokens,
    route_expert,
    route_weight,
    gate_weight,
    up_weight,
    down_weight,
    gate_scale,
    up_scale,
    down_scale,
):
    tok_rows, model_width = tokens.shape
    groups = lax.axis_size("expert")
    cores = lax.axis_size("tensor")
    assert cores == 2
    local_experts = gate_weight.shape[0]
    experts = local_experts * groups
    half_width = model_width // cores
    z, core = lax.axis_index("expert"), lax.axis_index("tensor")
    both = ("expert", "tensor")
    while groups * tok_rows // parts > ROW_LIMIT and tok_rows % (2 * parts) == 0:
        parts *= 2
    tok = tok_rows // parts
    if groups > 4:
        gather_shares, matmul_runs = (1,), (1,)

    def other_core(value):
        return lax.ppermute(value, "tensor", [(0, 1), (1, 0)])

    def onward(value, ups, downs):
        pairs = [(2 * i, 2 * (i + 1)) for i in ups] + [(2 * i + 1, 2 * (i - 1) + 1) for i in downs]
        return lax.ppermute(value, both, pairs)

    reach = jnp.where(core == 0, z, groups - 1 - z).astype(jnp.int32)

    weights_f = route_weight.astype(jnp.float32)
    mix = ROUTE_SCALE * weights_f / jnp.sum(weights_f, axis=1, keepdims=True)
    chosen = route_expert[:, :, None] == jnp.arange(experts, dtype=jnp.int32)[None, None, :]
    mix_rows = jnp.sum(jnp.where(chosen, mix[:, :, None], 0.0), axis=1)
    held, near, far = mix_rows, [mix_rows], []
    for s in range(1, groups):
        held = onward(held, range(s - 1, groups - 1), range(1, groups - s + 1))
        near.append(held)
        far.append(other_core(held))
    mix_all = jnp.stack(
        [near[0]]
        + [jnp.where(reach >= p, near[p], far[groups - p - 1]) for p in range(1, groups)]
    )
    mix_all = lax.dynamic_slice_in_dim(mix_all, z * local_experts, local_experts, 2)

    chunks = split_units(model_width, gather_shares)
    ret_chunks = split_units(half_width, return_shares)
    outs = []
    for part in range(parts):
        row0 = part * tok
        direct = [[] for _ in chunks]
        passed = [[] for _ in chunks]
        for k, (at, w) in enumerate(chunks):
            held = tokens[row0 : row0 + tok, at : at + w]
            for s in range(1, groups):
                held = onward(held, range(s - 1, groups - 1), range(1, groups - s + 1))
                direct[k].append(held)
                passed[k].append(other_core(held))
        sums, done = None, 0
        for i, run in enumerate(matmul_runs):
            last = i == len(matmul_runs) - 1
            ks = range(done, min(done + run, len(chunks)))
            sums = gate_up(
                reach.reshape(1),
                tokens,
                [direct[k] for k in ks],
                [passed[k] for k in ks],
                (gate_weight, up_weight),
                (gate_scale, up_scale),
                sums,
                row0,
                tok,
                chunks[done][0],
                [chunks[k][1] for k in ks],
                last,
                3584,
            )
            done += run
        hidden = sums
        mix_part = mix_all[:, row0 : row0 + tok].reshape(groups * tok, local_experts)
        pieces = []
        for k, cols in enumerate(ret_chunks):
            own, keep, send = down(
                hidden, down_weight, down_scale, mix_part, groups, cores, tok, cols
            )
            other = other_core(send)

            def ahead_at(j):
                return keep[j].astype(jnp.float32) + other[j].astype(jnp.float32)

            if k >= ring_from:
                total = ahead_at(groups - 2)
                for s in range(1, groups):
                    arrived = onward(
                        total.astype(jnp.bfloat16), range(0, s), range(groups - s, groups)
                    ).astype(jnp.float32)
                    total = arrived + (
                        ahead_at(groups - 2 - s) if s < groups - 1 else own.astype(jnp.float32)
                    )
            else:
                total, load = own.astype(jnp.float32), keep.astype(jnp.float32) + other.astype(jnp.float32)
                keep, other = lax.optimization_barrier((keep, other))
                ahead = keep.astype(jnp.float32) + other.astype(jnp.float32)
                for s in range(1, groups):
                    arrived = onward(load.astype(jnp.bfloat16), [s - 1], [groups - s])
                    arrived = arrived.astype(jnp.float32)
                    total = total + arrived[0]
                    load = ahead[: groups - s - 1] + arrived[1:]
            give = jnp.where(core == 0, total[1], total[0]).astype(jnp.bfloat16)
            stay = jnp.where(core == 0, total[0], total[1])
            got = other_core(give)
            pieces.append((stay + got.astype(jnp.float32)).astype(jnp.bfloat16))
        outs.append(jnp.concatenate(pieces, axis=1))
    return jnp.concatenate(outs, axis=0) if parts > 1 else outs[0]


def solution(mesh):
    in_specs = (
        P(("dp", "expert"), None),
        P(("dp", "expert"), None),
        P(("dp", "expert"), None),
        P("expert", None, "tensor"),
        P("expert", None, "tensor"),
        P("expert", "tensor", None),
        P("expert", "tensor"),
        P("expert", "tensor"),
        P("expert", None),
    )
    out_specs = P(("dp", "expert"), "tensor")
    plan = functools.partial(layer, GATHER, RUNS, RETURN, RING_FROM, PARTS)
    return jax.shard_map(plan, mesh=mesh, in_specs=in_specs, out_specs=out_specs, check_vma=False)
```
